32 devices in a mesh: group: 2 (over y), chan: 4 (over z), band: 2 (over x), beam: 2 (over core).
Axes of the slice: x: 2, y: 2, z: 4, core: 2. Of those that a mesh axis runs over, the one named last changes fastest.
Arguments:
- voltages: bfloat16 [2, 1024, 2, 8, 512], P(None, 'chan', 'band', None, 'group'), parts along dimension 4, may hold values from -6 to 6
- gains: float32 [2, 2, 8, 1024], P(None, 'band', 'chan'), may hold values from -5 to 5
- positions: float32 [3, 1024], replicated, may hold values from -4 to 4
- directions: float32 [3, 2048], P(None, ('group', 'beam')), parts along dimension 1, may hold values from -1 to 1
- antenna_row_lookup: int32 [1024], replicated, may hold values from 0 to 1023, each once
- chan_order: int32 [16], replicated, may hold values from 0 to 15, each once
- delays: int32 [4, 2, 8], replicated, may hold values from 0 to 31
Outputs:
- dedispersed: float32 [2, 8, 32, 2048], P('band', 'chan', None, ('group', 'beam')), parts along dimension 3
The draws below stay inside these ranges and needn't reach their ends.
There are 2 independent parts, one for each index of `group`. The reference program is written for one: setup_inputs(seed, part) draws one part's arguments, and reference() takes and returns one part's arrays. A program takes and returns all parts, laid end to end along the dimension named above; an argument that names none is the same for every part. Nothing has to cross between parts.
Inputs may be any that keep to these rules, and one draw needn't show every extreme that they name: `antenna_row_lookup`: each antenna appears once. `chan_order`: each frequency index appears once.
All inputs are finite; a program needn't handle non-finite values.
Results may differ from the reference program's by a relative error of at most 0.004.
Values may be sent and summed in bfloat16 or wider, within the bound.
A program may use at most 64 MiB of HBM per device.

```python
import math
import jax
import jax.numpy as jnp
from jax import lax

ANTENNA_COUNT = 1024
BEAMS = 1024
SAMPLE_COUNT = 256
INTEG = 8
FREQ_BAND_COUNT = 2
CHANNELS_PER_BAND = 8
CHANNEL_COUNT = 16
TB = 32
ROUNDS = 4


def place_ends(values, key, low, largest):
    extent = values.shape
    index_at = [jax.random.randint(jax.random.fold_in(key, axis), (), 0, extent[axis]) for axis in range(len(extent))]
    values = values.at[tuple(index_at)].set(low)
    longest = extent.index(max(extent))
    index_at[longest] = (index_at[longest] + 1) % extent[longest]
    return values.at[tuple(index_at)].set(largest)


def block_scale(key, shape, cuts, smallest, top_value):
    gain, own = 1.0, jax.random.fold_in(key, 6)
    for position, shards_of in cuts:
        steps = jnp.exp(jax.random.uniform(jax.random.fold_in(own, position), (shards_of,), jnp.float32, smallest / len(cuts), top_value / len(cuts)))
        gain = gain * jnp.repeat(steps, shape[position] // shards_of).reshape([-1 if axis == position else 1 for axis in range(len(shape))])
    return gain


def bell_draw(stream_key, shape, scale, bound, split=(), dtype=jnp.bfloat16):
    values = scale * jax.random.normal(stream_key, shape, jnp.float32)
    if split:
        values = values * block_scale(stream_key, shape, split, -0.22, 0.18)
    return jnp.clip(values, -bound, bound).astype(dtype)


def setup_inputs(seed: int = 0, part: int = 0) -> dict:
    splits = jax.random.split(jax.random.key(seed), 8)
    part_keys = jax.random.split(jax.random.fold_in(splits[7], part), 8)
    voltages = bell_draw(part_keys[0], (2, ANTENNA_COUNT, FREQ_BAND_COUNT, CHANNELS_PER_BAND, SAMPLE_COUNT), 1.0, 6.0, ((1, 4), (2, 2)))
    gains = bell_draw(splits[1], (2, FREQ_BAND_COUNT, CHANNELS_PER_BAND, ANTENNA_COUNT), 0.7, 5.0, ((1, 2), (2, 4)), jnp.float32)
    positions = jnp.clip(jax.random.uniform(splits[2], (3, ANTENNA_COUNT), jnp.float32, -4.0, 4.0), -4.0, 4.0)
    directions = jnp.clip(jax.random.uniform(part_keys[3], (3, BEAMS), jnp.float32, -1.0, 1.0) * block_scale(part_keys[3], (3, BEAMS), ((1, 2),), -0.4, 0.0), -1.0, 1.0)
    antenna_row_lookup = jax.random.permutation(splits[4], ANTENNA_COUNT).astype(jnp.int32)
    chan_order = jax.random.permutation(splits[5], CHANNEL_COUNT).astype(jnp.int32)
    delays = place_ends(jax.random.randint(splits[6], (ROUNDS, FREQ_BAND_COUNT, CHANNELS_PER_BAND), 0, TB), jax.random.fold_in(splits[6], 1), 0, TB - 1).astype(jnp.int32)
    return {"voltages": voltages, "gains": gains, "positions": positions, "directions": directions, "antenna_row_lookup": antenna_row_lookup, "chan_order": chan_order, "delays": delays}


def roll_rows(state, shifts):
    length = state.shape[1]
    doubled = jnp.concatenate([state, state], axis=1)

    def one_row(row, shift):
        return lax.dynamic_slice_in_dim(row, length - shift, length, 0)
    return jax.vmap(one_row)(doubled, shifts)

def pair_round(state, shifts, stride):
    count, length, width = state.shape
    grouped = state.reshape(count // (2 * stride), 2, stride, length, width)
    lower = jnp.broadcast_to(grouped[:, 0:1], grouped.shape).reshape(state.shape)
    upper = jnp.broadcast_to(grouped[:, 1:2], grouped.shape).reshape(state.shape)
    return lower + roll_rows(upper, shifts)

def beam_weights(gain_pair, freq, pos_rows, dirs):
    geometry = pos_rows[0][:, None] * dirs[0][None, :]
    geometry = geometry + pos_rows[1][:, None] * dirs[1][None, :]
    geometry = geometry + pos_rows[2][:, None] * dirs[2][None, :]
    phase = (2.0 * math.pi * freq)[:, None, None] * geometry[None]
    cosine = jnp.cos(phase)
    sine = jnp.sin(phase)
    g_re = gain_pair[0][:, :, None]
    g_im = gain_pair[1][:, :, None]
    factor = 1.0 / math.sqrt(pos_rows.shape[1])
    w_re = ((g_re * cosine + g_im * sine) * factor).astype(jnp.bfloat16)
    w_im = ((g_im * cosine - g_re * sine) * factor).astype(jnp.bfloat16)
    upper_rows = jnp.concatenate([w_re, w_im], axis=2)
    lower_rows = jnp.concatenate([-w_im, w_re], axis=2)
    return jnp.stack([upper_rows, lower_rows], axis=1)

def integrate(power, chans):
    count, samples, width = power.shape
    binned = lax.optimization_barrier(jnp.mean(power.reshape(count, samples // INTEG, INTEG, width), axis=2))
    centred = binned - lax.optimization_barrier(jnp.mean(binned, axis=1, keepdims=True))
    return centred * (1.0 / math.sqrt(chans))

def reference(voltages, gains, positions, directions, antenna_row_lookup, chan_order, delays):
    pos_rows = positions[:, antenna_row_lookup]
    freq = 1.0 + chan_order.astype(jnp.float32) / CHANNEL_COUNT
    voltage_cube = jnp.moveaxis(voltages.reshape(2, ANTENNA_COUNT, CHANNEL_COUNT, SAMPLE_COUNT), 2, 0)
    gain_table_rows = jnp.moveaxis(gains.reshape(2, CHANNEL_COUNT, ANTENNA_COUNT), 1, 0)

    def one_channel(items):
        vol_c, gain_c, freq_c = items
        weights = beam_weights(gain_c[:, None, :], freq_c[None], pos_rows, directions)[0].astype(jnp.float32)
        beams = jnp.einsum('pat,paq->tq', vol_c.astype(jnp.float32), weights)
        half = beams.shape[1] // 2
        power = beams[:, :half] * beams[:, :half] + beams[:, half:] * beams[:, half:]
        return integrate(power[None], CHANNEL_COUNT)[0]
    level = lax.map(one_channel, (voltage_cube, gain_table_rows, freq))
    flat_delays = delays.reshape(ROUNDS, CHANNEL_COUNT)
    for bit in range(ROUNDS):
        level = pair_round(level, flat_delays[bit], 1 << bit)
    return level.reshape(FREQ_BAND_COUNT, CHANNELS_PER_BAND, TB, BEAMS)
```

```python
import functools
import math

import jax
import jax.numpy as jnp
from jax import lax
from jax.experimental import pallas as pl
from jax.experimental.pallas import tpu as pltpu
from jax.sharding import PartitionSpec as P

INTEG = 8
MESH = pl.DeviceIdType.MESH
SIN = (4.44288283, -7.30824114, 3.60628867, -0.84576206, 0.10920298)
COS = (1.4142135, -6.97885095, 5.73946031, -1.88355744, 0.31068696)
CUTS = 2


def horner(coefs, x):
    total = jnp.full_like(x, coefs[-1])
    for coef in coefs[-2::-1]:
        total = total * x + coef
    return total


def roll_down(state, shift):
    rows = state.shape[0]
    for bit in range(rows.bit_length() - 1):
        moved = pltpu.roll(state, 1 << bit, 0)
        state = jnp.where((shift >> bit) & 1 == 1, moved, state)
    return state


def kernel(
    zs, bands, total, order_ref, delay_ref, volt_ref, gain_ref, pos_ref, dirs_ref, lookup_ref, out_ref,
    send, recv, table, weights, acc, other_dirs, level, other_level, tx, rx, select,
    v_send, v_recv, d_send, d_recv, l_send, l_recv, t_send, t_recv,
):
    z = lax.axis_index("chan")
    x = lax.axis_index("band")
    core = lax.axis_index("beam")
    antennas = lookup_ref.shape[1]
    local_ants = antennas // zs
    in_band = 2 * zs
    half = dirs_ref.shape[1]
    bins = level.shape[1]
    z_bits = zs.bit_length() - 1
    x_bits = bands.bit_length() - 1
    slot = x * in_band + z * 2 + core

    barrier = pltpu.get_barrier_semaphore()
    for d in range(1, zs):
        pl.semaphore_signal(barrier, inc=1, device_id={"chan": (z + d) % zs}, device_id_type=MESH)
    pl.semaphore_signal(barrier, inc=1, device_id={"beam": 1 - core}, device_id_type=MESH)
    for bit in range(x_bits):
        pl.semaphore_signal(barrier, inc=1, device_id={"band": x ^ (1 << bit)}, device_id_type=MESH)

    ants = select.shape[0] // zs
    rows = lax.broadcasted_iota(jnp.int32, select.shape, 0)
    cols = lax.broadcasted_iota(jnp.int32, select.shape, 1)
    ant_bits = ants.bit_length() - 1
    wanted = (rows & (ants - 1)) * in_band + (rows >> ant_bits) * 2 + core
    select[...] = jnp.where(cols == wanted, 1.0, 0.0).astype(jnp.bfloat16)
    for part in range(2):
        for block in range(local_ants // ants):
            lines = volt_ref[part, block * ants * in_band : (block + 1) * ants * in_band, :]
            picked = jnp.dot(select[...], lines, preferred_element_type=jnp.float32).astype(jnp.bfloat16)
            start = part * local_ants + block * ants
            for dest in range(zs):
                send[dest, start : start + ants, :] = picked[dest * ants : (dest + 1) * ants]

    pl.semaphore_wait(barrier, zs + x_bits)
    copies = []
    for d in range(1, zs):
        dest = (z + d) % zs
        copy = pltpu.make_async_remote_copy(
            src_ref=send.at[dest], dst_ref=recv.at[d - 1], send_sem=v_send.at[d - 1], recv_sem=v_recv.at[d - 1],
            device_id={"chan": dest}, device_id_type=MESH,
        )
        copy.start()
        copies.append(copy)
    dirs_copy = pltpu.make_async_remote_copy(
        src_ref=dirs_ref, dst_ref=other_dirs, send_sem=d_send, recv_sem=d_recv,
        device_id={"beam": 1 - core}, device_id_type=MESH,
    )
    dirs_copy.start()

    freq = 1.0 + order_ref[slot].astype(jnp.float32) / total
    pos = pos_ref[...]
    top = pos.astype(jnp.bfloat16)
    rest = pos - top.astype(jnp.float32)
    middle = rest.astype(jnp.bfloat16)
    last = (rest - middle.astype(jnp.float32)).astype(jnp.bfloat16)
    wide = 256
    for block in range(antennas // wide):
        span = slice(block * wide, (block + 1) * wide)
        row_no = lax.broadcasted_iota(jnp.int32, (antennas, wide), 0)
        hot = jnp.where(row_no == lookup_ref[:, span], 1.0, 0.0).astype(jnp.bfloat16)
        gathered = jnp.dot(top, hot, preferred_element_type=jnp.float32)
        gathered = gathered + jnp.dot(middle, hot, preferred_element_type=jnp.float32)
        gathered = gathered + jnp.dot(last, hot, preferred_element_type=jnp.float32)
        lines = gathered * freq + gain_ref[:, span] * (1.0 / math.sqrt(antennas))
        table[span, :] = lines.T

    tile = 16

    def fill(side, dirs):
        def step(index, carry):
            d = index // (local_ants // tile)
            row = (index % (local_ants // tile)) * tile
            source = (z - d + zs) % zs
            info = table[pl.ds(pl.multiple_of(source * local_ants + row, tile), tile), :]
            turns = info[:, 0:1] * dirs[0:1, :] + info[:, 1:2] * dirs[1:2, :] + info[:, 2:3] * dirs[2:3, :]
            r = turns - lax.round(turns, lax.RoundingMethod.TO_NEAREST_EVEN)
            sq = r * r
            s = r * horner(SIN, sq)
            c = horner(COS, sq)
            sine = s * c
            cosine = 1.0 - s * s
            g_re, g_im = info[:, 3:4], info[:, 4:5]
            w_re = (g_re * cosine + g_im * sine).astype(jnp.bfloat16)
            w_im = (g_im * cosine - g_re * sine).astype(jnp.bfloat16)
            columns = slice(side * half, (side + 1) * half)
            at = pl.multiple_of(row, tile)
            weights[d, pl.ds(at, tile), columns] = w_im
            weights[d, pl.ds(local_ants + at, tile), columns] = w_re
            weights[d, pl.ds(2 * local_ants + at, tile), columns] = -w_im
            return carry

        lax.fori_loop(0, antennas // tile, step, 0)

    fill(0, dirs_ref)
    dirs_copy.wait()
    fill(1, other_dirs)

    contract = (((0,), (0,)), ((), ()))
    for d in range(zs):
        if d == 0:
            block = send[z]
        else:
            copies[d - 1].wait()
            block = recv[d - 1]
        re = lax.dot_general(
            block, weights[d, local_ants : 3 * local_ants, :], contract, preferred_element_type=jnp.float32
        )
        im = lax.dot_general(
            block, weights[d, : 2 * local_ants, :], contract, preferred_element_type=jnp.float32
        )
        if d == 0:
            acc[0], acc[1] = re, im
        elif d < zs - 1:
            acc[0] += re
            acc[1] += im
        else:
            re = acc[0] + re
            im = acc[1] + im
    power = re * re + im * im
    binned = jnp.mean(power.reshape(bins, INTEG, 2 * half), axis=1)
    centred = (binned - jnp.mean(binned, axis=0, keepdims=True)) * (1.0 / math.sqrt(total))
    level[0] = centred[:, :half]
    level[1] = centred[:, half:]

    swap = pltpu.make_async_remote_copy(
        src_ref=level.at[1], dst_ref=other_level, send_sem=l_send, recv_sem=l_recv,
        device_id={"beam": 1 - core}, device_id_type=MESH,
    )
    swap.start()
    swap.wait()
    base = x * in_band + z * 2
    width = half // CUTS
    rounds = [("chan", bit) for bit in range(z_bits)] + [("band", bit) for bit in range(x_bits)]

    def send_round(no, cut, states):
        axis, bit = rounds[no]
        for ch in range(2):
            tx[no, cut, ch] = states[ch].astype(jnp.bfloat16)
        copy = pltpu.make_async_remote_copy(
            src_ref=tx.at[no, cut], dst_ref=rx.at[no, cut], send_sem=t_send.at[no, cut], recv_sem=t_recv.at[no, cut],
            device_id={axis: (z if axis == "chan" else x) ^ (1 << bit)}, device_id_type=MESH,
        )
        copy.start()
        return copy

    held, flights = [], []
    for cut in range(CUTS):
        span = slice(cut * width, (cut + 1) * width)
        mine, theirs = level[0, :, span], other_level[:, span]
        lower = jnp.where(core == 0, mine, theirs)
        upper = jnp.where(core == 0, theirs, mine)
        states = [lower + roll_down(upper, delay_ref[0, base + ch]) for ch in range(2)]
        held.append(states)
        flights.append(send_round(0, cut, states))
    for no, (axis, bit) in enumerate(rounds):
        place = z if axis == "chan" else x
        is_upper = (place >> bit) & 1 == 1
        for cut in range(CUTS):
            flights[cut].wait()
            states = []
            for ch in range(2):
                mine, theirs = held[cut][ch], rx[no, cut, ch].astype(jnp.float32)
                lower = jnp.where(is_upper, theirs, mine)
                upper = jnp.where(is_upper, mine, theirs)
                states.append(lower + roll_down(upper, delay_ref[no + 1, base + ch]))
            held[cut] = states
            if no + 1 < len(rounds):
                flights[cut] = send_round(no + 1, cut, states)
            else:
                for ch in range(2):
                    out_ref[ch, :, cut * width : (cut + 1) * width] = states[ch]


def shards(voltages, gains, positions, directions, antenna_row_lookup, chan_order, delays):
    zs = lax.axis_size("chan")
    bands = lax.axis_size("band")
    in_band = voltages.shape[3]
    total = in_band * bands
    antennas = positions.shape[1]
    local_ants = voltages.shape[1]
    samples = voltages.shape[4]
    bins = samples // INTEG
    half = directions.shape[1]
    ants = max(16, 256 // in_band)
    rounds = delays.shape[0]
    steps = rounds - 1
    core = lax.axis_index("beam")
    lines = voltages.reshape(2, local_ants * in_band, samples)
    gain = lax.dynamic_index_in_dim(gains[:, 0], core, 1, keepdims=False)
    gain = jnp.pad(gain, ((3, 3), (0, 0)))
    pos = jnp.pad(positions, ((0, 5), (0, 0)))
    dma = pltpu.SemaphoreType.DMA
    smem = pl.BlockSpec(memory_space=pltpu.SMEM)
    vmem = pl.BlockSpec(memory_space=pltpu.VMEM)
    out = pl.pallas_call(
        functools.partial(kernel, zs, bands, total),
        out_shape=jax.ShapeDtypeStruct((2, bins, half), jnp.float32),
        in_specs=[smem, smem, vmem, vmem, vmem, vmem, vmem],
        out_specs=vmem,
        scratch_shapes=[
            pltpu.VMEM((zs, 2 * local_ants, samples), jnp.bfloat16),
            pltpu.VMEM((zs - 1, 2 * local_ants, samples), jnp.bfloat16),
            pltpu.VMEM((antennas, 8), jnp.float32),
            pltpu.VMEM((zs, 3 * local_ants, 2 * half), jnp.bfloat16),
            pltpu.VMEM((2, samples, 2 * half), jnp.float32),
            pltpu.VMEM(directions.shape, jnp.float32),
            pltpu.VMEM((2, bins, half), jnp.float32),
            pltpu.VMEM((bins, half), jnp.float32),
            pltpu.VMEM((steps, CUTS, 2, bins, half // CUTS), jnp.bfloat16),
            pltpu.VMEM((steps, CUTS, 2, bins, half // CUTS), jnp.bfloat16),
            pltpu.VMEM((zs * ants, ants * in_band), jnp.bfloat16),
            dma((zs - 1,)),
            dma((zs - 1,)),
            dma(()),
            dma(()),
            dma(()),
            dma(()),
            dma((steps, CUTS)),
            dma((steps, CUTS)),
        ],
        compiler_params=pltpu.CompilerParams(
            collective_id=0, has_side_effects=True, vmem_limit_bytes=48 * 1024 * 1024
        ),
    )(
        chan_order, delays.reshape(rounds, total), lines, gain, pos, directions, antenna_row_lookup.reshape(1, antennas)
    )
    return out.reshape(1, 2, bins, half)


def solution(mesh):
    placed = (
        P(None, "chan", "band", None, "group"),
        P(None, "band", "chan", None),
        P(),
        P(None, ("group", "beam")),
        P(),
        P(),
        P(),
    )
    return jax.shard_map(
        shards,
        mesh=mesh,
        in_specs=placed,
        out_specs=P("band", "chan", None, ("group", "beam")),
        check_vma=False,
    )
```

```python
import functools
import math

import jax
import jax.numpy as jnp
from jax import lax
from jax.experimental import pallas as pl
from jax.experimental.pallas import tpu as pltpu
from jax.sharding import PartitionSpec as P

INTEG = 8
MESH = pl.DeviceIdType.MESH
SIN = (4.44288283, -7.30824114, 3.60628867, -0.84576206, 0.10920298)
COS = (1.4142135, -6.97885095, 5.73946031, -1.88355744, 0.31068696)


def horner(coefs, x):
    total = jnp.full_like(x, coefs[-1])
    for coef in coefs[-2::-1]:
        total = total * x + coef
    return total


def roll_down(state, shift):
    rows = state.shape[0]
    for bit in range(rows.bit_length() - 1):
        moved = pltpu.roll(state, 1 << bit, 0)
        state = jnp.where((shift >> bit) & 1 == 1, moved, state)
    return state


def kernel(
    zs, bands, total, order_in, delay_in, volt_in, gain_in, pos_in, dirs_in, lookup_in, out_ref,
    order_ref, delay_ref, volt_ref, gain_ref, pos_ref, dirs_ref, lookup_ref,
    send, recv, lines, table, weights, acc, other_dirs, tx, state, fin_tx, fin_rx, rx, select,
    load, v_send, v_recv, d_send, d_recv, l_send, l_recv, f_send, f_recv,
):
    z = lax.axis_index("chan")
    x = lax.axis_index("band")
    core = lax.axis_index("beam")
    antennas = lookup_ref.shape[1]
    local_ants = antennas // zs
    in_band = 2 * zs
    half = dirs_ref.shape[1]
    bins, chunk = rx.shape[1:]
    slot = x * in_band + z * 2 + core
    peers = [(h, dz, dx) for dx in range(bands) for dz in range(zs) for h in range(2)][1:]

    def at(h, dz, dx):
        return {"beam": core if h == 0 else 1 - core, "chan": (z + dz) % zs, "band": (x + dx) % bands}

    loads = [
        pltpu.make_async_copy(src, dst, load.at[no])
        for no, (src, dst) in enumerate(
            (
                (volt_in.at[0], volt_ref.at[0]), (volt_in.at[1], volt_ref.at[1]), (dirs_in, dirs_ref),
                (lookup_in, lookup_ref), (pos_in, pos_ref), (gain_in, gain_ref), (order_in, order_ref),
                (delay_in, delay_ref),
            )
        )
    ]
    for copy in loads:
        copy.start()
    barrier = pltpu.get_barrier_semaphore()
    for peer in peers:
        pl.semaphore_signal(barrier, inc=1, device_id=at(*peer), device_id_type=MESH)

    ants = select.shape[0] // zs
    rows = lax.broadcasted_iota(jnp.int32, select.shape, 0)
    cols = lax.broadcasted_iota(jnp.int32, select.shape, 1)
    ant_bits = ants.bit_length() - 1
    wanted = (rows & (ants - 1)) * in_band + (rows >> ant_bits) * 2 + core
    select[...] = jnp.where(cols == wanted, 1.0, 0.0).astype(jnp.bfloat16)
    copies = {}
    for part in range(2):
        loads[part].wait()
        for block in range(local_ants // ants):
            rows_in = volt_ref[part, block * ants * in_band : (block + 1) * ants * in_band, :]
            picked = jnp.dot(select[...], rows_in, preferred_element_type=jnp.float32).astype(jnp.bfloat16)
            start = part * local_ants + block * ants
            for dest in range(zs):
                send[dest, start : start + ants, :] = picked[dest * ants : (dest + 1) * ants]
        if part == 0:
            pl.semaphore_wait(barrier, len(peers))
        span = slice(part * local_ants, (part + 1) * local_ants)
        for d in range(1, zs):
            dest = (z + d) % zs
            copies[d, part] = pltpu.make_async_remote_copy(
                src_ref=send.at[dest, span], dst_ref=recv.at[d - 1, span],
                send_sem=v_send.at[d - 1, part], recv_sem=v_recv.at[d - 1, part],
                device_id=at(0, d, 0), device_id_type=MESH,
            )
            copies[d, part].start()
    loads[2].wait()
    dirs_copy = pltpu.make_async_remote_copy(
        src_ref=dirs_ref, dst_ref=other_dirs, send_sem=d_send, recv_sem=d_recv,
        device_id=at(1, 0, 0), device_id_type=MESH,
    )
    dirs_copy.start()
    for copy in loads[3:]:
        copy.wait()

    freq = 1.0 + order_ref[slot].astype(jnp.float32) / total
    lines[...] = jnp.zeros_like(lines)
    lines[0:3, :] = pos_ref[...]
    pos = lines[...]
    top = pos.astype(jnp.bfloat16)
    rest = pos - top.astype(jnp.float32)
    middle = rest.astype(jnp.bfloat16)
    last = (rest - middle.astype(jnp.float32)).astype(jnp.bfloat16)
    wide = 256
    for block in range(antennas // wide):
        span = slice(block * wide, (block + 1) * wide)
        row_no = lax.broadcasted_iota(jnp.int32, (antennas, wide), 0)
        hot = jnp.where(row_no == lookup_ref[:, span], 1.0, 0.0).astype(jnp.bfloat16)
        gathered = jnp.dot(top, hot, preferred_element_type=jnp.float32)
        gathered = gathered + jnp.dot(middle, hot, preferred_element_type=jnp.float32)
        gathered = gathered + jnp.dot(last, hot, preferred_element_type=jnp.float32)
        lines[0:3, span] = gathered[0:3] * freq
        for part in range(2):
            own = jnp.where(core == 0, gain_ref[part, 0, 0:1, span], gain_ref[part, 0, 1:2, span])
            lines[3 + part : 4 + part, span] = own * (1.0 / math.sqrt(antennas))
        table[span, :] = lines[:, span].T

    tile = 16

    def fill(side, dirs):
        def step(index, carry):
            d = index // (local_ants // tile)
            row = (index % (local_ants // tile)) * tile
            source = (z - d + zs) % zs
            info = table[pl.ds(pl.multiple_of(source * local_ants + row, tile), tile), :]
            turns = info[:, 0:1] * dirs[0:1, :] + info[:, 1:2] * dirs[1:2, :] + info[:, 2:3] * dirs[2:3, :]
            r = turns - lax.round(turns, lax.RoundingMethod.TO_NEAREST_EVEN)
            sq = r * r
            s = r * horner(SIN, sq)
            c = horner(COS, sq)
            sine = s * c
            cosine = 1.0 - s * s
            g_re, g_im = info[:, 3:4], info[:, 4:5]
            w_re = (g_re * cosine + g_im * sine).astype(jnp.bfloat16)
            w_im = (g_im * cosine - g_re * sine).astype(jnp.bfloat16)
            columns = slice(side * half, (side + 1) * half)
            first = pl.multiple_of(row, tile)
            weights[d, pl.ds(first, tile), columns] = w_im
            weights[d, pl.ds(local_ants + first, tile), columns] = w_re
            weights[d, pl.ds(2 * local_ants + first, tile), columns] = -w_im
            return carry

        lax.fori_loop(0, antennas // tile, step, 0, unroll=2)

    fill(0, dirs_ref)
    dirs_copy.wait()
    fill(1, other_dirs)

    contract = (((0,), (0,)), ((), ()))
    for d in range(zs):
        if d == 0:
            block = send[z]
        else:
            copies[d, 0].wait()
            copies[d, 1].wait()
            block = recv[d - 1]
        re = lax.dot_general(
            block, weights[d, local_ants : 3 * local_ants, :], contract, preferred_element_type=jnp.float32
        )
        im = lax.dot_general(
            block, weights[d, : 2 * local_ants, :], contract, preferred_element_type=jnp.float32
        )
        if d == 0:
            acc[0], acc[1] = re, im
        elif d < zs - 1:
            acc[0] += re
            acc[1] += im
        else:
            re = acc[0] + re
            im = acc[1] + im
    power = re * re + im * im
    binned = jnp.mean(power.reshape(bins, INTEG, 2 * half), axis=1)
    centred = (binned - jnp.mean(binned, axis=0, keepdims=True)) * (1.0 / math.sqrt(total))
    for h in range(2):
        for place in range(zs):
            start = h * half + place * chunk
            tx[h, place] = centred[:, start : start + chunk].astype(jnp.bfloat16)
    swaps = []
    for h, dz, dx in peers:
        copy = pltpu.make_async_remote_copy(
            src_ref=tx.at[h, (z + dz) % zs], dst_ref=rx.at[slot],
            send_sem=l_send.at[h, dz, dx], recv_sem=l_recv.at[h, dz, dx],
            device_id=at(h, dz, dx), device_id_type=MESH,
        )
        copy.start()
        swaps.append(copy)
    rx[slot] = tx[0, z]
    for copy in swaps:
        copy.wait()

    rounds = delay_ref.shape[0]

    def load_state(no, c):
        return rx[c].astype(jnp.float32) if no == 0 else state[no % 2, c]

    for no in range(rounds):
        stride = 1 << no

        def one(index, carry, no=no, stride=stride):
            c = index if no < rounds - 1 else x * in_band + index
            offset = (c // stride) % 2 * stride
            lower = load_state(no, c - offset)
            upper = load_state(no, c - offset + stride)
            shift = delay_ref[no, c // in_band, c % in_band]
            value = lower + roll_down(upper, shift)
            if no < rounds - 1:
                state[(no + 1) % 2, c] = value
            else:
                fin_tx[index // 2, index % 2] = value.astype(jnp.bfloat16)
            return carry

        count = total if no < rounds - 1 else in_band
        lax.fori_loop(0, count, one, 0, unroll=8)

    ends = []
    for d in range(1, zs):
        copy = pltpu.make_async_remote_copy(
            src_ref=fin_tx.at[(z + d) % zs], dst_ref=fin_rx.at[z], send_sem=f_send.at[d - 1],
            recv_sem=f_recv.at[d - 1], device_id=at(0, d, 0), device_id_type=MESH,
        )
        copy.start()
        ends.append(copy)
    fin_rx[z] = fin_tx[z]
    for copy in ends:
        copy.wait()
    for ch in range(2):
        parts = [fin_rx[source, ch].astype(jnp.float32) for source in range(zs)]
        out_ref[ch] = jnp.concatenate(parts, axis=1)


def shards(voltages, gains, positions, directions, antenna_row_lookup, chan_order, delays):
    zs = lax.axis_size("chan")
    bands = lax.axis_size("band")
    in_band = voltages.shape[3]
    total = in_band * bands
    antennas = positions.shape[1]
    local_ants = voltages.shape[1]
    samples = voltages.shape[4]
    bins = samples // INTEG
    half = directions.shape[1]
    ants = max(16, 256 // in_band)
    rounds = delays.shape[0]
    chunk = half // zs
    bf16, f32 = jnp.bfloat16, jnp.float32
    lines = voltages.reshape(2, local_ants * in_band, samples)
    lookup = antenna_row_lookup.reshape(1, antennas)
    dma = pltpu.SemaphoreType.DMA
    vmem = pltpu.VMEM
    out = pl.pallas_call(
        functools.partial(kernel, zs, bands, total),
        out_shape=jax.ShapeDtypeStruct((2, bins, half), f32),
        in_specs=[pl.BlockSpec(memory_space=pltpu.MemorySpace.HBM)] * 7,
        out_specs=pl.BlockSpec(memory_space=vmem),
        scratch_shapes=[
            pltpu.SMEM(chan_order.shape, jnp.int32),
            pltpu.SMEM(delays.shape, jnp.int32),
            vmem(lines.shape, bf16),
            vmem(gains.shape, f32),
            vmem(positions.shape, f32),
            vmem(directions.shape, f32),
            vmem(lookup.shape, jnp.int32),
            vmem((zs, 2 * local_ants, samples), bf16),
            vmem((zs - 1, 2 * local_ants, samples), bf16),
            vmem((8, antennas), f32),
            vmem((antennas, 8), f32),
            vmem((zs, 3 * local_ants, 2 * half), bf16),
            vmem((2, samples, 2 * half), f32),
            vmem(directions.shape, f32),
            vmem((2, zs, bins, chunk), bf16),
            vmem((2, total, bins, chunk), f32),
            vmem((zs, 2, bins, chunk), bf16),
            vmem((zs, 2, bins, chunk), bf16),
            vmem((total, bins, chunk), bf16),
            vmem((zs * ants, ants * in_band), bf16),
            dma((8,)),
            dma((zs - 1, 2)),
            dma((zs - 1, 2)),
            dma(()),
            dma(()),
            dma((2, zs, bands)),
            dma((2, zs, bands)),
            dma((zs - 1,)),
            dma((zs - 1,)),
        ],
        compiler_params=pltpu.CompilerParams(
            collective_id=0, has_side_effects=True, vmem_limit_bytes=56 * 1024 * 1024
        ),
    )(chan_order, delays, lines, gains, positions, directions, lookup)
    return out.reshape(1, 2, bins, half)


def solution(mesh):
    placed = (
        P(None, "chan", "band", None, "group"),
        P(None, "band", "chan", None),
        P(),
        P(None, ("group", "beam")),
        P(),
        P(),
        P(),
    )
    return jax.shard_map(
        shards,
        mesh=mesh,
        in_specs=placed,
        out_specs=P("band", "chan", None, ("group", "beam")),
        check_vma=False,
    )
```

```python
import functools
import math

import jax
import jax.numpy as jnp
from jax import lax
from jax.experimental import pallas as pl
from jax.experimental.pallas import tpu as pltpu
from jax.sharding import PartitionSpec as P

INTEG = 8
MESH = pl.DeviceIdType.MESH
SIN = (4.44288283, -7.30824114, 3.60628867, -0.84576206, 0.10920298)
COS = (1.4142135, -6.97885095, 5.73946031, -1.88355744, 0.31068696)


def horner(coefs, x):
    total = jnp.full_like(x, coefs[-1])
    for coef in coefs[-2::-1]:
        total = total * x + coef
    return total


def roll_down(state, shift):
    rows = state.shape[0]
    for bit in range(rows.bit_length() - 1):
        moved = pltpu.roll(state, 1 << bit, 0)
        state = jnp.where((shift >> bit) & 1 == 1, moved, state)
    return state


def pack(value, folds):
    rows = value.shape[0] // folds
    return jnp.concatenate([value[k * rows : (k + 1) * rows] for k in range(folds)], axis=1)


def unpack(value, folds):
    lanes = value.shape[1] // folds
    return jnp.concatenate([value[:, k * lanes : (k + 1) * lanes] for k in range(folds)], axis=0)


def kernel(
    zs, bands, total, cuts, folds, order_in, delay_in, volt_in, gain_in, pos_in, dirs_in, lookup_in, out_ref,
    order_ref, delay_ref, volt_ref, gain_ref, pos_ref, dirs_ref, lookup_ref,
    send, recv, lines, table, weights, acc, other_dirs, tx, state, fin_tx, fin_rx, rx, select,
    load, v_send, v_recv, d_send, d_recv, l_send, l_recv, f_send, f_recv,
):
    z = lax.axis_index("chan")
    x = lax.axis_index("band")
    core = lax.axis_index("beam")
    antennas = lookup_ref.shape[1]
    local_ants = antennas // zs
    in_band = 2 * zs
    half = dirs_ref.shape[1]
    bins, chunk = state.shape[2:]
    order = [zs // 2] + [d for d in range(1, zs) if d != zs // 2]
    spot = z * cuts + (x if cuts > 1 else 0)
    slot = x * in_band + z * 2 + core
    peers = [(h, dz, dx) for dx in range(bands) for dz in range(zs) for h in range(2)][1:]

    def at(h, dz, dx):
        return {"beam": core if h == 0 else 1 - core, "chan": (z + dz) % zs, "band": (x + dx) % bands}

    loads = [
        pltpu.make_async_copy(src, dst, load.at[no])
        for no, (src, dst) in enumerate(
            (
                (volt_in.at[0], volt_ref.at[0]), (volt_in.at[1], volt_ref.at[1]), (dirs_in, dirs_ref),
                (lookup_in, lookup_ref), (pos_in, pos_ref), (gain_in, gain_ref), (order_in, order_ref),
                (delay_in, delay_ref),
            )
        )
    ]
    for copy in loads:
        copy.start()
    barrier = pltpu.get_barrier_semaphore()
    for peer in peers:
        pl.semaphore_signal(barrier, inc=1, device_id=at(*peer), device_id_type=MESH)

    ants = select.shape[0] // zs
    rows = lax.broadcasted_iota(jnp.int32, select.shape, 0)
    cols = lax.broadcasted_iota(jnp.int32, select.shape, 1)
    ant_bits = ants.bit_length() - 1
    wanted = (rows & (ants - 1)) * in_band + (rows >> ant_bits) * 2 + core
    select[...] = jnp.where(cols == wanted, 1.0, 0.0).astype(jnp.bfloat16)
    copies = {}
    for part in range(2):
        loads[part].wait()
        for block in range(local_ants // ants):
            rows_in = volt_ref[part, block * ants * in_band : (block + 1) * ants * in_band, :]
            picked = jnp.dot(select[...], rows_in, preferred_element_type=jnp.float32).astype(jnp.bfloat16)
            start = part * local_ants + block * ants
            for dest in range(zs):
                send[dest, start : start + ants, :] = picked[dest * ants : (dest + 1) * ants]
        if part == 0:
            pl.semaphore_wait(barrier, len(peers))
        span = slice(part * local_ants, (part + 1) * local_ants)
        for d in order:
            dest = (z + d) % zs
            copies[d, part] = pltpu.make_async_remote_copy(
                src_ref=send.at[dest, span], dst_ref=recv.at[d - 1, span],
                send_sem=v_send.at[d - 1, part], recv_sem=v_recv.at[d - 1, part],
                device_id=at(0, d, 0), device_id_type=MESH,
            )
            copies[d, part].start()
    loads[2].wait()
    dirs_copy = pltpu.make_async_remote_copy(
        src_ref=dirs_ref, dst_ref=other_dirs, send_sem=d_send, recv_sem=d_recv,
        device_id=at(1, 0, 0), device_id_type=MESH,
    )
    dirs_copy.start()
    for copy in loads[3:]:
        copy.wait()

    freq = 1.0 + order_ref[slot].astype(jnp.float32) / total
    lines[...] = jnp.zeros_like(lines)
    lines[0:3, :] = pos_ref[...]
    pos = lines[...]
    top = pos.astype(jnp.bfloat16)
    rest = pos - top.astype(jnp.float32)
    middle = rest.astype(jnp.bfloat16)
    last = (rest - middle.astype(jnp.float32)).astype(jnp.bfloat16)
    wide = 256
    for block in range(antennas // wide):
        span = slice(block * wide, (block + 1) * wide)
        row_no = lax.broadcasted_iota(jnp.int32, (antennas, wide), 0)
        hot = jnp.where(row_no == lookup_ref[:, span], 1.0, 0.0).astype(jnp.bfloat16)
        gathered = jnp.dot(top, hot, preferred_element_type=jnp.float32)
        gathered = gathered + jnp.dot(middle, hot, preferred_element_type=jnp.float32)
        gathered = gathered + jnp.dot(last, hot, preferred_element_type=jnp.float32)
        lines[0:3, span] = gathered[0:3] * freq
        for part in range(2):
            own = jnp.where(core == 0, gain_ref[part, 0, 0:1, span], gain_ref[part, 0, 1:2, span])
            lines[3 + part : 4 + part, span] = own * (1.0 / math.sqrt(antennas))
        table[span, :] = lines[:, span].T

    tile = 16

    def fill(side, dirs):
        def step(index, carry):
            d = index // (local_ants // tile)
            row = (index % (local_ants // tile)) * tile
            source = (z - d + zs) % zs
            info = table[pl.ds(pl.multiple_of(source * local_ants + row, tile), tile), :]
            turns = info[:, 0:1] * dirs[0:1, :] + info[:, 1:2] * dirs[1:2, :] + info[:, 2:3] * dirs[2:3, :]
            r = turns - lax.round(turns, lax.RoundingMethod.TO_NEAREST_EVEN)
            sq = r * r
            s = r * horner(SIN, sq)
            c = horner(COS, sq)
            sine = s * c
            cosine = 1.0 - s * s
            g_re, g_im = info[:, 3:4], info[:, 4:5]
            w_re = (g_re * cosine + g_im * sine).astype(jnp.bfloat16)
            w_im = (g_im * cosine - g_re * sine).astype(jnp.bfloat16)
            columns = slice(side * half, (side + 1) * half)
            first = pl.multiple_of(row, tile)
            weights[d, pl.ds(first, tile), columns] = w_im
            weights[d, pl.ds(local_ants + first, tile), columns] = w_re
            weights[d, pl.ds(2 * local_ants + first, tile), columns] = -w_im
            return carry

        lax.fori_loop(0, antennas // tile, step, 0, unroll=4)

    fill(0, dirs_ref)
    dirs_copy.wait()
    fill(1, other_dirs)

    contract = (((0,), (0,)), ((), ()))
    for d in [0] + order:
        if d == 0:
            block = send[z]
        else:
            copies[d, 0].wait()
            copies[d, 1].wait()
            block = recv[d - 1]
        re = lax.dot_general(
            block, weights[d, local_ants : 3 * local_ants, :], contract, preferred_element_type=jnp.float32
        )
        im = lax.dot_general(
            block, weights[d, : 2 * local_ants, :], contract, preferred_element_type=jnp.float32
        )
        if d == 0:
            acc[0], acc[1] = re, im
        elif d != order[-1]:
            acc[0] += re
            acc[1] += im
        else:
            re = acc[0] + re
            im = acc[1] + im
    power = re * re + im * im
    binned = jnp.mean(power.reshape(bins, INTEG, 2 * half), axis=1)
    centred = (binned - jnp.mean(binned, axis=0, keepdims=True)) * (1.0 / math.sqrt(total))
    for h in range(2):
        for place in range(zs * cuts):
            start = h * half + place * chunk
            tx[h, place] = pack(centred[:, start : start + chunk], folds).astype(jnp.bfloat16)
    swaps = []
    for dz in order + [0]:
        for dx in range(bands):
            for h in range(2):
                if (h, dz, dx) == (0, 0, 0):
                    continue
                place = (z + dz) % zs * cuts + ((x + dx) % bands if cuts > 1 else 0)
                copy = pltpu.make_async_remote_copy(
                    src_ref=tx.at[h, place], dst_ref=rx.at[slot],
                    send_sem=l_send.at[h, dz, dx], recv_sem=l_recv.at[h, dz, dx],
                    device_id=at(h, dz, dx), device_id_type=MESH,
                )
                copy.start()
                swaps.append(copy)
    rx[slot] = tx[0, spot]
    for copy in swaps:
        copy.wait()

    rounds = delay_ref.shape[0]

    def load_state(no, c):
        return unpack(rx[c].astype(jnp.float32), folds) if no == 0 else state[no % 2, c]

    def merged(no, c):
        stride = 1 << no
        offset = (c // stride) % 2 * stride
        lower = load_state(no, c - offset)
        upper = load_state(no, c - offset + stride)
        return lower + roll_down(upper, delay_ref[no, c // in_band, c % in_band])

    for no in range(rounds - 1):

        def one(c, carry, no=no):
            state[(no + 1) % 2, c] = merged(no, c)
            return carry

        lax.fori_loop(0, total, one, 0, unroll=16)

    ends = []
    for dz, dx in [(dz, dx) for dz in order + [0] for dx in range(cuts)]:
        to_z, to_x = (z + dz) % zs, (x + dx) % bands
        place = to_z * cuts + (to_x if cuts > 1 else 0)
        for ch in range(2):
            value = merged(rounds - 1, to_x * in_band + 2 * to_z + ch)
            fin_tx[place, ch] = pack(value, folds).astype(jnp.bfloat16)
        if (dz, dx) != (0, 0):
            copy = pltpu.make_async_remote_copy(
                src_ref=fin_tx.at[place], dst_ref=fin_rx.at[spot], send_sem=f_send.at[dz, dx],
                recv_sem=f_recv.at[dz, dx], device_id=at(0, dz, dx), device_id_type=MESH,
            )
            copy.start()
            ends.append(copy)
    fin_rx[spot] = fin_tx[spot]
    for copy in ends:
        copy.wait()
    for ch in range(2):
        parts = [unpack(fin_rx[source, ch].astype(jnp.float32), folds) for source in range(zs * cuts)]
        out_ref[ch] = jnp.concatenate(parts, axis=1)


def shards(voltages, gains, positions, directions, antenna_row_lookup, chan_order, delays):
    zs = lax.axis_size("chan")
    bands = lax.axis_size("band")
    in_band = voltages.shape[3]
    total = in_band * bands
    antennas = positions.shape[1]
    local_ants = voltages.shape[1]
    samples = voltages.shape[4]
    bins = samples // INTEG
    half = directions.shape[1]
    ants = max(16, 256 // in_band)
    rounds = delays.shape[0]
    cuts = 1
    chunk = half // (zs * cuts)
    folds = 2 if 2 * chunk == 128 else 1
    packed = (bins // folds, chunk * folds)
    bf16, f32 = jnp.bfloat16, jnp.float32
    lines = voltages.reshape(2, local_ants * in_band, samples)
    lookup = antenna_row_lookup.reshape(1, antennas)
    dma = pltpu.SemaphoreType.DMA
    vmem = pltpu.VMEM
    out = pl.pallas_call(
        functools.partial(kernel, zs, bands, total, cuts, folds),
        out_shape=jax.ShapeDtypeStruct((2, bins, half), f32),
        in_specs=[pl.BlockSpec(memory_space=pltpu.MemorySpace.HBM)] * 7,
        out_specs=pl.BlockSpec(memory_space=vmem),
        scratch_shapes=[
            pltpu.SMEM(chan_order.shape, jnp.int32),
            pltpu.SMEM(delays.shape, jnp.int32),
            vmem(lines.shape, bf16),
            vmem(gains.shape, f32),
            vmem(positions.shape, f32),
            vmem(directions.shape, f32),
            vmem(lookup.shape, jnp.int32),
            vmem((zs, 2 * local_ants, samples), bf16),
            vmem((zs - 1, 2 * local_ants, samples), bf16),
            vmem((8, antennas), f32),
            vmem((antennas, 8), f32),
            vmem((zs, 3 * local_ants, 2 * half), bf16),
            vmem((2, samples, 2 * half), f32),
            vmem(directions.shape, f32),
            vmem((2, zs * cuts, *packed), bf16),
            vmem((2, total, bins, chunk), f32),
            vmem((zs * cuts, 2, *packed), bf16),
            vmem((zs * cuts, 2, *packed), bf16),
            vmem((total, *packed), bf16),
            vmem((zs * ants, ants * in_band), bf16),
            dma((8,)),
            dma((zs - 1, 2)),
            dma((zs - 1, 2)),
            dma(()),
            dma(()),
            dma((2, zs, bands)),
            dma((2, zs, bands)),
            dma((zs, cuts)),
            dma((zs, cuts)),
        ],
        compiler_params=pltpu.CompilerParams(
            collective_id=0, has_side_effects=True, vmem_limit_bytes=56 * 1024 * 1024
        ),
    )(chan_order, delays, lines, gains, positions, directions, lookup)
    return out.reshape(1, 2, bins, half)


def solution(mesh):
    placed = (
        P(None, "chan", "band", None, "group"),
        P(None, "band", "chan", None),
        P(),
        P(None, ("group", "beam")),
        P(),
        P(),
        P(),
    )
    return jax.shard_map(
        shards,
        mesh=mesh,
        in_specs=placed,
        out_specs=P("band", "chan", None, ("group", "beam")),
        check_vma=False,
    )
```

```python
import functools
import math

import jax
import jax.numpy as jnp
from jax import lax
from jax.experimental import pallas as pl
from jax.experimental.pallas import tpu as pltpu
from jax.sharding import PartitionSpec as P

INTEG = 8
MESH = pl.DeviceIdType.MESH
SIN = (4.44288283, -7.30824114, 3.60628867, -0.84576206, 0.10920298)
COS = (1.4142135, -6.97885095, 5.73946031, -1.88355744, 0.31068696)


def horner(coefs, x):
    total = jnp.full_like(x, coefs[-1])
    for coef in coefs[-2::-1]:
        total = total * x + coef
    return total


def roll_down(state, shift):
    rows = state.shape[0]
    for bit in range(rows.bit_length() - 1):
        moved = pltpu.roll(state, 1 << bit, 0)
        state = jnp.where((shift >> bit) & 1 == 1, moved, state)
    return state


def pack(value, folds):
    rows = value.shape[0] // folds
    return jnp.concatenate([value[k * rows : (k + 1) * rows] for k in range(folds)], axis=1)


def unpack(value, folds):
    lanes = value.shape[1] // folds
    return jnp.concatenate([value[:, k * lanes : (k + 1) * lanes] for k in range(folds)], axis=0)


def kernel(
    zs, bands, total, cuts, folds, order_in, delay_in, volt_in, gain_in, pos_in, dirs_in, lookup_in, out_ref,
    order_ref, delay_ref, volt_ref, gain_ref, pos_ref, dirs_ref, lookup_ref,
    send, recv, lines, table, weights, acc, other_dirs, tx, state, fin_tx, fin_rx, rx, select,
    load, v_send, v_recv, d_send, d_recv, l_send, l_recv, f_send, f_recv,
):
    z = lax.axis_index("chan")
    x = lax.axis_index("band")
    core = lax.axis_index("beam")
    antennas = lookup_ref.shape[1]
    local_ants = antennas // zs
    in_band = 2 * zs
    half = dirs_ref.shape[1]
    bins, chunk = state.shape[2:]
    order = [zs // 2] + [d for d in range(1, zs) if d != zs // 2]
    spot = z * cuts + (x if cuts > 1 else 0)
    slot = x * in_band + z * 2 + core
    peers = [(h, dz, dx) for dx in range(bands) for dz in range(zs) for h in range(2)][1:]

    def at(h, dz, dx):
        return {"beam": core if h == 0 else 1 - core, "chan": (z + dz) % zs, "band": (x + dx) % bands}

    loads = [
        pltpu.make_async_copy(src, dst, load.at[no])
        for no, (src, dst) in enumerate(
            (
                (volt_in.at[0], volt_ref.at[0]), (volt_in.at[1], volt_ref.at[1]), (dirs_in, dirs_ref),
                (lookup_in, lookup_ref), (pos_in, pos_ref), (gain_in, gain_ref), (order_in, order_ref),
                (delay_in, delay_ref),
            )
        )
    ]
    for copy in loads:
        copy.start()
    barrier = pltpu.get_barrier_semaphore()
    for peer in peers:
        pl.semaphore_signal(barrier, inc=1, device_id=at(*peer), device_id_type=MESH)

    ants = select.shape[0] // zs
    rows = lax.broadcasted_iota(jnp.int32, select.shape, 0)
    cols = lax.broadcasted_iota(jnp.int32, select.shape, 1)
    ant_bits = ants.bit_length() - 1
    wanted = (rows & (ants - 1)) * in_band + (rows >> ant_bits) * 2 + core
    select[...] = jnp.where(cols == wanted, 1.0, 0.0).astype(jnp.bfloat16)
    copies = {}
    for part in range(2):
        loads[part].wait()
        for block in range(local_ants // ants):
            rows_in = volt_ref[part, block * ants * in_band : (block + 1) * ants * in_band, :]
            picked = jnp.dot(select[...], rows_in, preferred_element_type=jnp.float32).astype(jnp.bfloat16)
            start = part * local_ants + block * ants
            for dest in range(zs):
                send[dest, start : start + ants, :] = picked[dest * ants : (dest + 1) * ants]
        if part == 0:
            pl.semaphore_wait(barrier, len(peers))
        span = slice(part * local_ants, (part + 1) * local_ants)
        for d in order:
            dest = (z + d) % zs
            copies[d, part] = pltpu.make_async_remote_copy(
                src_ref=send.at[dest, span], dst_ref=recv.at[d - 1, span],
                send_sem=v_send.at[d - 1, part], recv_sem=v_recv.at[d - 1, part],
                device_id=at(0, d, 0), device_id_type=MESH,
            )
            copies[d, part].start()
    loads[2].wait()
    dirs_copy = pltpu.make_async_remote_copy(
        src_ref=dirs_ref, dst_ref=other_dirs, send_sem=d_send, recv_sem=d_recv,
        device_id=at(1, 0, 0), device_id_type=MESH,
    )
    dirs_copy.start()
    for copy in loads[3:]:
        copy.wait()

    freq = 1.0 + order_ref[slot].astype(jnp.float32) / total
    lines[...] = jnp.zeros_like(lines)
    lines[0:3, :] = pos_ref[...]
    pos = lines[...]
    top = pos.astype(jnp.bfloat16)
    rest = pos - top.astype(jnp.float32)
    middle = rest.astype(jnp.bfloat16)
    last = (rest - middle.astype(jnp.float32)).astype(jnp.bfloat16)
    wide = 256
    for block in range(antennas // wide):
        span = slice(block * wide, (block + 1) * wide)
        row_no = lax.broadcasted_iota(jnp.int32, (antennas, wide), 0)
        hot = jnp.where(row_no == lookup_ref[:, span], 1.0, 0.0).astype(jnp.bfloat16)
        gathered = jnp.dot(top, hot, preferred_element_type=jnp.float32)
        gathered = gathered + jnp.dot(middle, hot, preferred_element_type=jnp.float32)
        gathered = gathered + jnp.dot(last, hot, preferred_element_type=jnp.float32)
        lines[0:3, span] = gathered[0:3] * freq
        for part in range(2):
            own = jnp.where(core == 0, gain_ref[part, 0, 0:1, span], gain_ref[part, 0, 1:2, span])
            lines[3 + part : 4 + part, span] = own * (1.0 / math.sqrt(antennas))
        table[span, :] = lines[:, span].T

    tile = 16

    def fill(side, dirs):
        def step(index, carry):
            d = index // (local_ants // tile)
            row = (index % (local_ants // tile)) * tile
            source = (z - d + zs) % zs
            info = table[pl.ds(pl.multiple_of(source * local_ants + row, tile), tile), :]
            turns = info[:, 0:1] * dirs[0:1, :] + info[:, 1:2] * dirs[1:2, :] + info[:, 2:3] * dirs[2:3, :]
            r = turns - lax.round(turns, lax.RoundingMethod.TO_NEAREST_EVEN)
            sq = r * r
            s = r * horner(SIN, sq)
            c = horner(COS, sq)
            sine = s * c
            cosine = 1.0 - s * s
            g_re, g_im = info[:, 3:4], info[:, 4:5]
            w_re = (g_re * cosine + g_im * sine).astype(jnp.bfloat16)
            w_im = (g_im * cosine - g_re * sine).astype(jnp.bfloat16)
            columns = slice(side * half, (side + 1) * half)
            first = pl.multiple_of(row, tile)
            weights[d, pl.ds(first, tile), columns] = w_im
            weights[d, pl.ds(local_ants + first, tile), columns] = w_re
            weights[d, pl.ds(2 * local_ants + first, tile), columns] = -w_im
            return carry

        lax.fori_loop(0, antennas // tile, step, 0, unroll=4)

    fill(0, dirs_ref)
    dirs_copy.wait()
    fill(1, other_dirs)

    contract = (((0,), (0,)), ((), ()))
    for d in [0] + order:
        if d == 0:
            block = send[z]
        else:
            copies[d, 0].wait_recv()
            copies[d, 1].wait_recv()
            block = recv[d - 1]
        re = lax.dot_general(
            block, weights[d, local_ants : 3 * local_ants, :], contract, preferred_element_type=jnp.float32
        )
        im = lax.dot_general(
            block, weights[d, : 2 * local_ants, :], contract, preferred_element_type=jnp.float32
        )
        if d == 0:
            acc[0], acc[1] = re, im
        elif d != order[-1]:
            acc[0] += re
            acc[1] += im
        else:
            re = acc[0] + re
            im = acc[1] + im
    power = re * re + im * im
    binned = jnp.mean(power.reshape(bins, INTEG, 2 * half), axis=1)
    centred = (binned - jnp.mean(binned, axis=0, keepdims=True)) * (1.0 / math.sqrt(total))
    for h in range(2):
        for place in range(zs * cuts):
            start = h * half + place * chunk
            tx[h, place] = pack(centred[:, start : start + chunk], folds).astype(jnp.bfloat16)
    swaps = []
    for dz in order + [0]:
        for dx in range(bands):
            for h in range(2):
                if (h, dz, dx) == (0, 0, 0):
                    continue
                place = (z + dz) % zs * cuts + ((x + dx) % bands if cuts > 1 else 0)
                copy = pltpu.make_async_remote_copy(
                    src_ref=tx.at[h, place], dst_ref=rx.at[slot],
                    send_sem=l_send.at[h, dz, dx], recv_sem=l_recv.at[h, dz, dx],
                    device_id=at(h, dz, dx), device_id_type=MESH,
                )
                copy.start()
                swaps.append(copy)
    rx[slot] = tx[0, spot]
    for copy in swaps:
        copy.wait_recv()

    rounds = delay_ref.shape[0]

    def load_state(no, c):
        return unpack(rx[c].astype(jnp.float32), folds) if no == 0 else state[no % 2, c]

    def merged(no, c):
        stride = 1 << no
        offset = (c // stride) % 2 * stride
        lower = load_state(no, c - offset)
        upper = load_state(no, c - offset + stride)
        return lower + roll_down(upper, delay_ref[no, c // in_band, c % in_band])

    for no in range(rounds - 1):

        def one(c, carry, no=no):
            state[(no + 1) % 2, c] = merged(no, c)
            return carry

        lax.fori_loop(0, total, one, 0, unroll=16)

    ends = []
    for dz, dx in [(dz, dx) for dz in order + [0] for dx in range(cuts)]:
        to_z, to_x = (z + dz) % zs, (x + dx) % bands
        place = to_z * cuts + (to_x if cuts > 1 else 0)
        for ch in range(2):
            value = merged(rounds - 1, to_x * in_band + 2 * to_z + ch)
            fin_tx[place, ch] = pack(value, folds).astype(jnp.bfloat16)
        if (dz, dx) != (0, 0):
            copy = pltpu.make_async_remote_copy(
                src_ref=fin_tx.at[place], dst_ref=fin_rx.at[spot], send_sem=f_send.at[dz, dx],
                recv_sem=f_recv.at[dz, dx], device_id=at(0, dz, dx), device_id_type=MESH,
            )
            copy.start()
            ends.append(copy)
    fin_rx[spot] = fin_tx[spot]
    for copy in ends:
        copy.wait_recv()
    for ch in range(2):
        parts = [unpack(fin_rx[source, ch].astype(jnp.float32), folds) for source in range(zs * cuts)]
        out_ref[ch] = jnp.concatenate(parts, axis=1)
    for copy in [*copies.values(), *swaps, *ends]:
        copy.wait_send()


def shards(voltages, gains, positions, directions, antenna_row_lookup, chan_order, delays):
    zs = lax.axis_size("chan")
    bands = lax.axis_size("band")
    in_band = voltages.shape[3]
    total = in_band * bands
    antennas = positions.shape[1]
    local_ants = voltages.shape[1]
    samples = voltages.shape[4]
    bins = samples // INTEG
    half = directions.shape[1]
    ants = max(16, 256 // in_band)
    rounds = delays.shape[0]
    cuts = 1
    chunk = half // (zs * cuts)
    folds = 2 if 2 * chunk == 128 else 1
    packed = (bins // folds, chunk * folds)
    bf16, f32 = jnp.bfloat16, jnp.float32
    lines = voltages.reshape(2, local_ants * in_band, samples)
    lookup = antenna_row_lookup.reshape(1, antennas)
    dma = pltpu.SemaphoreType.DMA
    vmem = pltpu.VMEM
    out = pl.pallas_call(
        functools.partial(kernel, zs, bands, total, cuts, folds),
        out_shape=jax.ShapeDtypeStruct((2, bins, half), f32),
        in_specs=[pl.BlockSpec(memory_space=pltpu.MemorySpace.HBM)] * 7,
        out_specs=pl.BlockSpec(memory_space=vmem),
        scratch_shapes=[
            pltpu.SMEM(chan_order.shape, jnp.int32),
            pltpu.SMEM(delays.shape, jnp.int32),
            vmem(lines.shape, bf16),
            vmem(gains.shape, f32),
            vmem(positions.shape, f32),
            vmem(directions.shape, f32),
            vmem(lookup.shape, jnp.int32),
            vmem((zs, 2 * local_ants, samples), bf16),
            vmem((zs - 1, 2 * local_ants, samples), bf16),
            vmem((8, antennas), f32),
            vmem((antennas, 8), f32),
            vmem((zs, 3 * local_ants, 2 * half), bf16),
            vmem((2, samples, 2 * half), f32),
            vmem(directions.shape, f32),
            vmem((2, zs * cuts, *packed), bf16),
            vmem((2, total, bins, chunk), f32),
            vmem((zs * cuts, 2, *packed), bf16),
            vmem((zs * cuts, 2, *packed), bf16),
            vmem((total, *packed), bf16),
            vmem((zs * ants, ants * in_band), bf16),
            dma((8,)),
            dma((zs - 1, 2)),
            dma((zs - 1, 2)),
            dma(()),
            dma(()),
            dma((2, zs, bands)),
            dma((2, zs, bands)),
            dma((zs, cuts)),
            dma((zs, cuts)),
        ],
        compiler_params=pltpu.CompilerParams(
            collective_id=0, has_side_effects=True, vmem_limit_bytes=56 * 1024 * 1024
        ),
    )(chan_order, delays, lines, gains, positions, directions, lookup)
    return out.reshape(1, 2, bins, half)


def solution(mesh):
    placed = (
        P(None, "chan", "band", None, "group"),
        P(None, "band", "chan", None),
        P(),
        P(None, ("group", "beam")),
        P(),
        P(),
        P(),
    )
    return jax.shard_map(
        shards,
        mesh=mesh,
        in_specs=placed,
        out_specs=P("band", "chan", None, ("group", "beam")),
        check_vma=False,
    )
```
